32 devices in a mesh: row: 8 (over z, core), col: 4 (over y, x).
Axes of the slice: x: 2, y: 2, z: 4, core: 2. Of those that a mesh axis runs over, the one named last changes fastest.
Arguments:
- eigenvectors: float32 [4096, 512], P('row', 'col'), may hold values from -6 to 6
- aligned_vectors: float32 [2, 4096, 256], P(None, 'row', 'col'), may hold values from -0.3 to 1, as said below
- straddle_vectors: float32 [2, 4096, 256], P(None, 'row', 'col'), may hold values from -0.3 to 1, as said below
Outputs:
- transformed: float32 [4096, 512], P('row', 'col')
The draws below stay inside these ranges and needn't reach their ends.
Inputs may be any that keep to these rules, and one draw needn't show every extreme that they name: `aligned_vectors`: within each block of 512 rows, column i is 1 in the block's row i and 0 in the rows above it. `straddle_vectors`: within each straddling block of the steps, column i is 1 in the block's row i and 0 in the rows above it.
All inputs are finite; a program needn't handle non-finite values.
Results may differ from the reference program's by a relative error of at most 0.00027.
Values sent between devices are 32-bit elements; how exact they have to be, the bound alone decides.
No kernel may reach another device: no remote copies, remote signals or barrier semaphores. Data moves between devices by JAX's collectives and lax.ppermute only.
A program may use at most 128 MiB of HBM per device.

```python
import jax
import jax.numpy as jnp
from jax import lax

NB = 256
SWEEPS = 2
ORDER = 4096
EIGVECS = 512
N_ROW = 8


def householder_columns(key, local_rows):
    column_ids = jnp.arange(NB)
    noise = 0.05 * jax.random.truncated_normal(key, -6.0, 6.0, (SWEEPS, ORDER, NB), jnp.float32)
    on_diagonal = local_rows[:, None] == column_ids[None, :]
    above_diagonal = local_rows[:, None] < column_ids[None, :]
    values = jnp.where(on_diagonal, 1.0, jnp.where(above_diagonal, 0.0, noise))
    return values.astype(jnp.float32)


def draw_aligned_vectors(key, part):
    local_rows = jnp.arange(ORDER) % (2 * NB)
    return householder_columns(jax.random.fold_in(key, 11), local_rows)


def draw_straddle_vectors(key, part):
    global_rows = jnp.arange(ORDER)
    within = global_rows % (2 * NB)
    local_rows = jnp.where(within < NB, jnp.where(global_rows < NB, within, within + NB), within - NB)
    return householder_columns(jax.random.fold_in(key, 23), local_rows)


def block_scale(rng, extent, shards, low, high):
    level, own = 1.0, jax.random.fold_in(rng, 6)
    for axis_at, parts in shards:
        heights = jnp.exp(jax.random.uniform(jax.random.fold_in(own, axis_at), (parts,), jnp.float32, low / len(shards), high / len(shards)))
        level = level * jnp.repeat(heights, extent[axis_at] // parts).reshape([-1 if axis == axis_at else 1 for axis in range(len(extent))])
    return level


def normal_values(stream_key, extent, deviation, most, shards=(), held_as=jnp.bfloat16):
    entries = jax.random.normal(stream_key, extent, jnp.float32) * deviation
    if len(shards) > 0:
        entries = block_scale(stream_key, extent, shards, -0.22, 0.18) * entries
    return jnp.clip(entries, min=-most, max=most).astype(held_as)


def setup_inputs(seed: int = 0) -> dict:
    seeds = jax.random.split(jax.random.key(seed), 4)
    eigenvectors = normal_values(seeds[0], (ORDER, EIGVECS), 1.0, 6.0, ((0, 8), (1, 4)), jnp.float32)
    aligned_vectors = draw_aligned_vectors(jax.random.fold_in(seeds[3], 71), 0)
    straddle_vectors = draw_straddle_vectors(jax.random.fold_in(seeds[3], 71), 0)
    return dict(eigenvectors=eigenvectors, aligned_vectors=aligned_vectors, straddle_vectors=straddle_vectors)


def matmul(left_side, right_side):
    return jnp.dot(left_side, right_side, precision=lax.Precision.HIGHEST, preferred_element_type=jnp.float32)


def square_product(left_side, right_side):
    return jnp.matmul(left_side, right_side, precision=lax.Precision.HIGHEST)


def cross_product(left_side, right_side):
    return lax.dot_general(left_side, right_side, (((0,), (0,)), ((), ())), precision=lax.Precision.HIGHEST, preferred_element_type=jnp.float32)


def small_inverse(upper_form):
    order_now = upper_form.shape[-1]
    diagonal_now = jnp.diagonal(upper_form, axis1=-2, axis2=-1)
    nilpotent = jnp.triu(upper_form, 1) / diagonal_now[..., :, None]
    identity_matrix = jnp.eye(order_now, dtype=upper_form.dtype)
    result = identity_matrix - nilpotent
    powered = nilpotent
    for level in range((order_now - 1).bit_length() - 1):
        powered = square_product(powered, powered)
        result = square_product(result, identity_matrix + powered)
    return result / diagonal_now[..., None, :]


def upper_inverse(upper_form):
    order_now = upper_form.shape[-1]
    if order_now <= 32:
        return small_inverse(upper_form)
    halfway = order_now // 2
    upper_left = upper_inverse(upper_form[..., :halfway, :halfway])
    lower_right = upper_inverse(upper_form[..., halfway:, halfway:])
    top_right = -square_product(square_product(upper_left, upper_form[..., :halfway, halfway:]), lower_right)
    bottom_left = jnp.zeros_like(top_right)
    top_rows = jnp.concatenate([upper_left, top_right], axis=-1)
    bottom_rows = jnp.concatenate([bottom_left, lower_right], axis=-1)
    return jnp.concatenate([top_rows, bottom_rows], axis=-2)


def triangle_factor(gram_matrix):
    upper_form = jnp.triu(gram_matrix, 1) + jnp.diag(0.5 * jnp.diag(gram_matrix))
    return upper_inverse(upper_form)


def reflect(row_slab, vectors, factor):
    return row_slab - matmul(vectors, matmul(factor, cross_product(vectors, row_slab)))


def reference(eigenvectors, aligned_vectors, straddle_vectors):
    half_rows = NB
    block_span = 2 * NB
    current = eigenvectors
    for sweep_index in range(SWEEPS):
        aligned_now = aligned_vectors[sweep_index]
        straddle_now = straddle_vectors[sweep_index]
        for device_row in range(N_ROW - 1, -1, -1):
            block_start = device_row * block_span
            top_start = block_start + half_rows
            top_vectors = straddle_now[top_start:top_start + half_rows]
            top_slab = current[top_start:top_start + half_rows]
            gram_matrix = cross_product(top_vectors, top_vectors)
            partial_value = cross_product(top_vectors, top_slab)
            if device_row + 1 < N_ROW:
                bottom_start = block_start + block_span
                bottom_vectors = straddle_now[bottom_start:bottom_start + half_rows]
                bottom_slab = current[bottom_start:bottom_start + half_rows]
                gram_matrix = gram_matrix + cross_product(bottom_vectors, bottom_vectors)
                partial_value = partial_value + cross_product(bottom_vectors, bottom_slab)
            coeffs = matmul(triangle_factor(gram_matrix), partial_value)
            current = current.at[top_start:top_start + half_rows].set(top_slab - matmul(top_vectors, coeffs))
            if device_row + 1 < N_ROW:
                current = current.at[bottom_start:bottom_start + half_rows].set(bottom_slab - matmul(bottom_vectors, coeffs))
            block_vectors = aligned_now[block_start:block_start + block_span]
            block_factor = triangle_factor(cross_product(block_vectors, block_vectors))
            current = current.at[block_start:block_start + block_span].set(reflect(current[block_start:block_start + block_span], block_vectors, block_factor))
        first_vectors = straddle_now[:half_rows]
        first_factor = triangle_factor(cross_product(first_vectors, first_vectors))
        current = current.at[:half_rows].set(reflect(current[:half_rows], first_vectors, first_factor))
    return current
```

```python
import functools

import jax
import jax.numpy as jnp
from jax import lax
from jax.experimental import pallas as pl
from jax.experimental.pallas import tpu as pltpu
from jax.sharding import PartitionSpec as P

F32 = jnp.float32
BF16 = jnp.bfloat16
BASE_BLOCK = 32


def split(value):
    high = value.astype(BF16)
    return high, (value - high.astype(F32)).astype(BF16)


def raw_dot(left, right, transposed):
    dims = (((1,), (1 if transposed else 0,)), ((), ()))
    return lax.dot_general(left, right, dims, preferred_element_type=F32)


def product(left, right, transposed=False):
    left = left if isinstance(left, tuple) else split(left)
    right = right if isinstance(right, tuple) else split(right)
    return (
        raw_dot(left[0], right[0], transposed)
        + raw_dot(left[0], right[1], transposed)
        + raw_dot(left[1], right[0], transposed)
    )


def cut(pair, rows=slice(None), lanes=slice(None)):
    return pair[0][rows, lanes], pair[1][rows, lanes]


def lower_inverses(grams):
    order = grams[0].shape[0]
    base = min(BASE_BLOCK, order)
    rows = lax.broadcasted_iota(jnp.int32, (order, order), 0)
    lanes = lax.broadcasted_iota(jnp.int32, (order, order), 1)
    identity = jnp.where(rows == lanes, 1.0, 0.0).astype(F32)
    strict = [jnp.where(rows > lanes, gram, 0.0) for gram in grams]
    across = [2.0 / jnp.sum(gram * identity, axis=0, keepdims=True) for gram in grams]
    along = [2.0 / jnp.sum(gram * identity, axis=1, keepdims=True) for gram in grams]
    same = rows // base == lanes // base
    nilpotent = [jnp.where(same, low * scale, 0.0) for low, scale in zip(strict, across)]
    result = [identity - value for value in nilpotent]
    powered = [split(value) for value in nilpotent]
    for level in range((base - 1).bit_length() - 1):
        squares = [product(value, value) for value in powered]
        powered = [split(value) for value in squares]
        result = [
            now + product(now, value) for now, value in zip(result, powered)
        ]
    result = [now * scale for now, scale in zip(result, along)]
    size = base
    while size < order:
        here = (rows // (2 * size) == lanes // (2 * size)) & (rows // size != lanes // size)
        parts = [split(now) for now in result]
        inner = [
            product(part, jnp.where(here, low, 0.0)) for part, low in zip(parts, strict)
        ]
        result = [
            now - product(value, part) for now, value, part in zip(result, inner, parts)
        ]
        size *= 2
    return result


def place(pieces, index_ref, first, target, width):
    for at, (piece, sweeps) in enumerate(pieces):
        start = pl.multiple_of(index_ref[first + at] * width, width)
        for sweep, source in sweeps:
            target[sweep, pl.ds(start, width), :] = piece[source]


def gram_kernel(layout, width, half, index_ref, *refs):
    count = len(layout)
    pieces = [(refs[at], layout[at]) for at in range(count)]
    matrix_ref, wide_ref, inner_ref, outer_ref = refs[count:]
    place(pieces, index_ref, 4, wide_ref, width)
    even = index_ref[0] == 0
    sweeps = wide_ref.shape[0]
    for sweep in range(sweeps):
        whole = split(wide_ref[sweep])
        below, above = cut(whole, lanes=slice(0, half)), cut(whole, lanes=slice(half, None))
        gram_below, gram_above = product(below, below, True), product(above, above, True)
        at = slice(sweep * half, (sweep + 1) * half)
        inner_ref[at, :] = jnp.where(even, gram_above, gram_below)
        outer_ref[at, :] = jnp.where(even, gram_below, gram_above)
        if sweep == 0:
            lower_rows = jnp.transpose(matrix_ref[half:, :])
            first = product(lower_rows, above, True)
            inner_ref[sweeps * half :, :] = first
            outer_ref[sweeps * half :, :] = first


def local_kernel(layout, width, half, index_ref, *refs):
    count = len(layout)
    pieces = [(refs[at], layout[at]) for at in range(count)]
    (
        matrix_ref, straddle_ref, inner_ref, inner_got_ref, outer_ref, outer_got_ref,
        wide_ref, step_ref, up_ref, now_ref, coeff_ref, factor_ref, square_ref,
    ) = refs[count:]
    place(pieces, index_ref, 4, wide_ref, width)
    parity = index_ref[0]
    even = parity == 0
    outside = jnp.where(index_ref[1] == 0, 1.0, 0.0)
    columns = matrix_ref.shape[1]
    grams = []
    for sweep in range(2):
        at = slice(sweep * half, (sweep + 1) * half)
        aligned = split(wide_ref[sweep])
        grams.append(inner_ref[at, :] + inner_got_ref[at, :])
        grams.append(outer_ref[at, :] + outside * outer_got_ref[at, :])
        grams.append(product(aligned, aligned, True))
    factors = lower_inverses(grams)
    for sweep in range(2):
        square_ref[sweep, parity] = factors[3 * sweep]
        square_ref[sweep, 1 - parity] = factors[3 * sweep + 1]
    top = slice(2 * half, 2 * half + columns)
    own_first = inner_ref[top, :]
    got_first = jnp.where(even, outside * outer_got_ref[top, :], inner_got_ref[top, :])

    current = jnp.transpose(matrix_ref[...])
    upper, lower = current[:, :half], current[:, half:]
    blank = jnp.zeros((half, half), F32)

    def pieces_of(sweep):
        straddle, aligned = split(straddle_ref[sweep]), split(wide_ref[sweep])
        return (
            cut(straddle, lanes=slice(0, half)), cut(straddle, lanes=slice(half, None)),
            cut(aligned, lanes=slice(0, half)), cut(aligned, lanes=slice(half, None)),
        )

    below, above, aligned_up, aligned_low = pieces_of(0)
    factor_above, factor_below = split(square_ref[0, 0]), split(square_ref[0, 1])
    factor_aligned = split(factors[2])
    through = split(product(above, aligned_low, True))
    onward = split(product(aligned_up, below, True))
    seen = product(upper, aligned_up, True) + product(lower, aligned_low, True)
    raw = product(upper, below, True)
    outer = jnp.concatenate([product(own_first, factor_above), square_ref[0, 0]], axis=0)
    outer_pair = split(outer)
    inside = jnp.concatenate([seen, blank], axis=0) - product(outer_pair, through)
    coeffs = split(product(inside, factor_aligned))
    carry = jnp.concatenate([raw, blank], axis=0) - product(coeffs, onward)
    step_ref[0:half, :] = carry[columns:]
    step_ref[3 * half : 3 * half + columns, :] = carry[:columns]
    back = split(
        product(
            jnp.concatenate([carry[:columns] + got_first, carry[columns:]], axis=0), factor_below
        )
    )
    upper = (
        jnp.concatenate([upper, blank], axis=0) - product(coeffs, aligned_up) - product(back, below)
    )
    lower = (
        jnp.concatenate([lower, blank], axis=0)
        - product(outer_pair, above)
        - product(coeffs, aligned_low)
    )
    now_ref[:, :half] = upper
    now_ref[:, half:] = lower

    below, above, aligned_up, aligned_low = pieces_of(1)
    factor_above = split(square_ref[1, 0])
    factor_aligned = split(factors[5])
    factor_ref[...] = square_ref[1, 1]
    through = split(product(above, aligned_low, True))
    onward = split(product(aligned_up, below, True))
    upper, lower = split(upper), split(lower)
    first = product(lower, above, True)
    up_ref[...] = first
    seen = product(upper, aligned_up, True) + product(lower, aligned_low, True)
    raw = product(upper, below, True)
    outer = jnp.concatenate([product(first, factor_above), square_ref[1, 0]], axis=0)
    inside = jnp.concatenate([seen, blank], axis=0) - product(outer, through)
    coeffs = product(inside, factor_aligned)
    carry = jnp.concatenate([raw, blank], axis=0) - product(coeffs, onward)
    coeff_ref[:, 0:half] = outer
    coeff_ref[:, half : 2 * half] = coeffs
    coeff_ref[:, 2 * half :] = carry
    step_ref[half : 2 * half, :] = carry[columns : columns + half]
    step_ref[2 * half : 3 * half, :] = carry[columns + half :]
    step_ref[3 * half + columns :, :] = carry[:columns]


def compose_kernel(half, index_ref, own_ref, got_ref, chain_ref, start_ref, both_ref):
    parity = index_ref[0]
    both_ref[parity] = own_ref[...]
    both_ref[1 - parity] = got_ref[...]
    columns = start_ref.shape[0] * 2
    part = columns // 2

    def block(core, at):
        return split(both_ref[core, at * half : (at + 1) * half, :])

    even0, even_mix, even1 = (block(0, at) for at in range(3))
    odd0, odd_mix, odd1 = (block(1, at) for at in range(3))
    chain_ref[0:half, :] = product(odd0, even0)
    chain_ref[half : 2 * half, :] = product(odd0, even_mix) + product(odd_mix, even1)
    chain_ref[2 * half :, :] = product(odd1, even1)

    def rows(core, sweep):
        start = pl.multiple_of(3 * half + sweep * columns + parity * part, 8)
        return both_ref[core, pl.ds(start, part), :]

    odd_first = split(rows(1, 0))
    start_ref[:, :half] = rows(0, 0) + product(odd_first, even0)
    start_ref[:, half:] = (
        rows(0, 1) + product(odd_first, even_mix) + product(rows(1, 1), even1)
    )


def hop_kernel(half, start_ref, chain_ref, got_ref, out_ref):
    zero, one = split(got_ref[:, :half]), split(got_ref[:, half:])
    out_ref[:, :half] = start_ref[:, :half] + product(zero, chain_ref[0:half, :])
    out_ref[:, half:] = (
        start_ref[:, half:]
        + product(zero, chain_ref[half : 2 * half, :])
        + product(one, chain_ref[2 * half :, :])
    )


def response_kernel(
    half, index_ref, own_ref, got_ref, up_ref, now_ref, coeff_ref, factor_ref, straddle_ref, wide_ref,
    base_ref, reply_ref,
):
    columns = base_ref.shape[0]
    keep = jnp.where(index_ref[2] == 0, 1.0, 0.0)
    given = split(keep * up_ref[columns:, :])
    first = jnp.concatenate(
        [own_ref[3 * half : 3 * half + columns, :], own_ref[0:half, :]], axis=0
    )
    offset = product(first, given)
    offset = jnp.concatenate(
        [offset[:columns] + keep * up_ref[:columns, :], offset[columns:]], axis=0
    )
    reach = columns + half
    carry = coeff_ref[:, 2 * half :]
    summed = jnp.concatenate([carry[:reach] + offset, carry[reach:]], axis=0)
    back = split(product(summed, factor_ref[...]))
    outer, coeffs = split(coeff_ref[:, 0:half]), split(coeff_ref[:, half : 2 * half])
    straddle, aligned = split(straddle_ref[0]), split(wide_ref[0])
    change_up = product(coeffs, cut(aligned, lanes=slice(0, half))) + product(
        back, cut(straddle, lanes=slice(0, half))
    )
    change_low = product(outer, cut(straddle, lanes=slice(half, None))) + product(
        coeffs, cut(aligned, lanes=slice(half, None))
    )
    change = jnp.concatenate([change_up, change_low], axis=1)
    base = now_ref[:columns, :] - change[:columns]
    middle = now_ref[columns:, :] - change[columns:reach]
    last = -change[reach:]

    @pl.when(index_ref[0] != 0)
    def _():
        base_ref[...] = base
        reply_ref[0:half, :] = middle
        reply_ref[half:, :] = last

    @pl.when(index_ref[0] == 0)
    def _():
        middle_pair, last_pair = split(middle), split(last)
        zero = split(
            jnp.concatenate([got_ref[3 * half : 3 * half + columns, :], got_ref[0:half, :]], axis=0)
        )
        one = split(
            jnp.concatenate([got_ref[3 * half + columns :, :], got_ref[half : 3 * half, :]], axis=0)
        )
        after_zero = product(zero, middle_pair)
        after_one = product(one, last_pair)
        base_ref[...] = base + after_zero[:columns] + after_one[:columns]
        reply_ref[0:half, :] = after_zero[columns:] + after_one[columns:reach]
        reply_ref[half:, :] = after_one[reach:]


def final_kernel(index_ref, own_ref, got_ref, base_ref, reply_ref, out_ref, carry_ref):
    parity = index_ref[0]
    carry_ref[parity] = own_ref[...]
    carry_ref[1 - parity] = got_ref[...]
    carry = jnp.concatenate([carry_ref[0], carry_ref[1]], axis=0)
    out_ref[...] = jnp.transpose(base_ref[...] + product(carry, reply_ref[...]))


def call(body, outs, *operands, scratch=(), flops=0):
    space = pl.BlockSpec(memory_space=pltpu.VMEM)
    first = [pl.BlockSpec(memory_space=pltpu.SMEM)] if operands[0].dtype == jnp.int32 else [space]
    shapes = [jax.ShapeDtypeStruct(shape, F32) for shape in outs]
    moved = sum(4 * operand.size for operand in operands) + sum(4 * shape.size for shape in shapes)
    return pl.pallas_call(
        body,
        out_shape=shapes,
        in_specs=first + [space] * (len(operands) - 1),
        out_specs=[space] * len(shapes),
        scratch_shapes=list(scratch),
        cost_estimate=pl.CostEstimate(flops=flops, bytes_accessed=moved, transcendentals=0),
    )(*operands)


def gathered(shard, axis):
    count = lax.axis_size(axis)
    me = lax.axis_index(axis)
    every = ((0, 0), (1, 1))
    if count == 4:
        swaps = [[(i, i ^ mask) for i in range(count)] for mask in (1, 2)]
        near = lax.ppermute(shard, axis, swaps[0])
        side = lax.ppermute(shard, axis, swaps[1])
        far_first = lax.ppermute(side[0:1], axis, swaps[0])
        far_second = lax.ppermute(near[1:2], axis, swaps[1])
        arrays = [shard, near, side, far_first, far_second]
        places = [me, me ^ 1, me ^ 2, me ^ 3, me ^ 3]
        return arrays, places, [every, every, every, ((0, 0),), ((1, 0),)]
    arrays, places, layout = [shard], [me], [every]
    for step in range(1, count):
        route = [((i + step) % count, i) for i in range(count)]
        arrays.append(lax.ppermute(shard, axis, route))
        places.append((me + step) % count)
        layout.append(every)
    return arrays, places, layout


def on_device(eigenvectors, aligned_vectors, straddle_vectors):
    aligned = jnp.swapaxes(aligned_vectors, 1, 2)
    straddle = jnp.swapaxes(straddle_vectors, 1, 2)
    sweeps, width, span = aligned.shape
    half = span // 2
    columns = eigenvectors.shape[1]
    part = columns // 2
    rows = lax.axis_size("row")
    row = lax.axis_index("row")
    chips = rows // 2

    straddle_parts, places, layout = gathered(straddle, "col")
    aligned_parts, _, _ = gathered(aligned, "col")
    parity = row % 2
    outside = jnp.where(parity == 0, row == 0, row == rows - 1)
    index = jnp.stack(
        [parity, outside.astype(jnp.int32), (row == 0).astype(jnp.int32), row]
        + [jnp.asarray(place, jnp.int32) for place in places]
    ).astype(jnp.int32)
    unit = 2 * half * half * half * 3

    wide_straddle, inner, outer = call(
        functools.partial(gram_kernel, layout, width, half),
        [(sweeps, half, span), (sweeps * half + columns, half), (sweeps * half + columns, half)],
        index, *straddle_parts, eigenvectors, flops=5 * unit,
    )
    inside_route = [(i, i ^ 1) for i in range(rows)]
    outside_route = [(i, (i - 1 if i % 2 == 0 else i + 1) % rows) for i in range(rows)]
    inner_got = lax.ppermute(inner, "row", inside_route)
    outer_got = lax.ppermute(outer, "row", outside_route)
    reach = columns + half
    wide_aligned, step, up, now, coeff, factor, _ = call(
        functools.partial(local_kernel, layout, width, half),
        [
            (sweeps, half, span), (3 * half + 2 * columns, half), (reach, half), (reach, span),
            (reach + half, 3 * half), (half, half), (2, 2, half, half),
        ],
        index, *aligned_parts, eigenvectors, wide_straddle, inner, inner_got, outer, outer_got,
        flops=140 * unit,
    )
    step_got = lax.ppermute(step, "row", inside_route)
    up_got = lax.ppermute(up, "row", [(i, i + 1) for i in range(rows - 1)])
    chain, start = call(
        functools.partial(compose_kernel, half),
        [(3 * half, half), (part, span)],
        index, step, step_got, scratch=[pltpu.VMEM((2,) + step.shape, F32)], flops=6 * unit,
    )
    down = [(i, i - 2) for i in range(2, rows)]
    carry = start
    for hop in range(chips - 1):
        got = lax.ppermute(carry, "row", down)
        if hop < chips - 2:
            (carry,) = call(
                functools.partial(hop_kernel, half), [(part, span)], start, chain, got, flops=unit
            )
    if chips == 1:
        got = jnp.zeros_like(start)
    base, reply = call(
        functools.partial(response_kernel, half),
        [(columns, span), (span, span)],
        index, step, step_got, up_got, now, coeff, factor, wide_straddle[1:], wide_aligned[1:],
        flops=30 * unit,
    )
    other = lax.ppermute(got, "row", inside_route)
    (result,) = call(
        final_kernel, [(span, columns)], index, got, other, base, reply,
        scratch=[pltpu.VMEM((2, part, span), F32)], flops=4 * unit,
    )
    return result


def solution(mesh):
    placed = (P("row", "col"), P(None, "row", "col"), P(None, "row", "col"))
    return jax.shard_map(
        on_device, mesh=mesh, in_specs=placed, out_specs=P("row", "col"), check_vma=False
    )
```

```python
import functools

import jax
import jax.numpy as jnp
from jax import lax
from jax.experimental import pallas as pl
from jax.experimental.pallas import tpu as pltpu
from jax.sharding import PartitionSpec as P


F32 = jnp.float32
BF16 = jnp.bfloat16
BASE_BLOCK = 32
LANES = 128
PAD = 8
VMEM_GRANT = 16 * 1024 * 1024


def split(value):
    high = value.astype(BF16)
    return high, (value - high.astype(F32)).astype(BF16)


def raw_dot(left, right, transposed):
    dims = (((1,), (1 if transposed else 0,)), ((), ()))
    return lax.dot_general(left, right, dims, preferred_element_type=F32)


def product(left, right, transposed=False):
    left = left if isinstance(left, tuple) else split(left)
    right = right if isinstance(right, tuple) else split(right)
    return (
        raw_dot(left[0], right[0], transposed)
        + raw_dot(left[0], right[1], transposed)
        + raw_dot(left[1], right[0], transposed)
    )


def cut(pair, rows=slice(None), lanes=slice(None)):
    return pair[0][rows, lanes], pair[1][rows, lanes]


def stack(*values):
    return jnp.concatenate(values, axis=0)


def beside(*values):
    return jnp.concatenate(values, axis=1)


def block_inverse(packed, base):
    done = []
    for start in range(0, packed.shape[1], LANES):
        entries = packed[:, start : start + LANES]
        rows = lax.broadcasted_iota(jnp.int32, entries.shape, 0)
        lanes = lax.broadcasted_iota(jnp.int32, entries.shape, 1)
        group = (lanes // base) * base
        value = jnp.where(rows == lanes - group, 1.0, 0.0).astype(F32)
        for step in range(base - 1):
            top = (step // 8) * 8
            factor = jnp.take_along_axis(entries[top:], (group + step)[top:], axis=1)
            changed = value[top:] - factor * value[step : step + 1]
            value = stack(value[:top], changed) if top else changed
        done.append(value)
    return beside(*done)


def small_inverse(strict, across, base):
    order = strict.shape[0]
    lanes = lax.broadcasted_iota(jnp.int32, (base, order), 1) // base
    packed = jnp.zeros((base, order), F32)
    for block in range(order // base):
        packed = jnp.where(lanes == block, strict[block * base : (block + 1) * base], packed)
    solved = block_inverse(packed * across, base)
    return stack(*[jnp.where(lanes == block, solved, 0.0) for block in range(order // base)])


def lower_inverses(stricts, diagonals):
    order = stricts[0].shape[0]
    base = min(BASE_BLOCK, order)
    rows = lax.broadcasted_iota(jnp.int32, (order, order), 0)
    lanes = lax.broadcasted_iota(jnp.int32, (order, order), 1)
    result = []
    for strict, diagonal in zip(stricts, diagonals):
        across = 2.0 / diagonal
        along = jnp.sum(jnp.where(rows == lanes, across, 0.0), axis=1, keepdims=True)
        result.append(small_inverse(strict, across, base) * along)
    size = base
    while 2 * size < order:
        here = (rows // (2 * size) == lanes // (2 * size)) & (rows // size != lanes // size)
        wholes = [split(now) for now in result]
        starts = range(0, order, 2 * size)
        odds = [
            tuple(stack(*[part[at + size : at + 2 * size] for at in starts]) for part in whole)
            for whole in wholes
        ]
        inner = [
            product(odd, jnp.where(here, strict, 0.0)) for odd, strict in zip(odds, stricts)
        ]
        outer = [product(value, whole) for value, whole in zip(inner, wholes)]
        merged = []
        for now, change in zip(result, outer):
            bands = []
            for number, at in enumerate(starts):
                bands.append(now[at : at + size])
                bands.append(
                    now[at + size : at + 2 * size] - change[number * size : (number + 1) * size]
                )
            merged.append(stack(*bands))
        result = merged
        size *= 2
    if size < order:
        wholes = [split(now) for now in result]
        low, high = slice(0, size), slice(size, None)
        inner = [
            product(cut(whole, high, high), strict[high, low])
            for whole, strict in zip(wholes, stricts)
        ]
        outer = [product(value, cut(whole, low, low)) for value, whole in zip(inner, wholes)]
        result = [
            stack(now[low], beside(-change, now[high, high]))
            for now, change in zip(result, outer)
        ]
    return result


def place(pieces, index_ref, first, target, width):
    for at, (piece, sweeps) in enumerate(pieces):
        start = pl.multiple_of(index_ref[first + at] * width, width)
        for sweep, source in sweeps:
            target[sweep, pl.ds(start, width), :] = piece[source]


def triangle(order):
    rows = lax.broadcasted_iota(jnp.int32, (order, order), 0)
    lanes = lax.broadcasted_iota(jnp.int32, (order, order), 1)
    return rows > lanes, rows == lanes


def pack_grams(target, pair, below, diagonal):
    half = pair[0].shape[0]
    target[0:half, :] = jnp.where(below, pair[0], pair[1])
    for at, gram in enumerate(pair):
        target[half + at : half + at + 1, :] = jnp.sum(
            jnp.where(diagonal, gram, 0.0), axis=0, keepdims=True
        )


def gram_kernel(layout, width, half, index_ref, *refs):
    count = len(layout)
    pieces = [(refs[at], layout[at]) for at in range(count)]
    matrix_ref, wide_ref, inner_ref, outer_ref = refs[count:]
    place(pieces, index_ref, 4, wide_ref, width)
    even = index_ref[0] == 0
    below, diagonal = triangle(half)
    lows, highs = [], []
    for sweep in range(2):
        whole = split(wide_ref[sweep])
        low, high = cut(whole, lanes=slice(0, half)), cut(whole, lanes=slice(half, None))
        lows.append(product(low, low, True))
        highs.append(product(high, high, True))
        if sweep == 0:
            first = product(jnp.transpose(matrix_ref[half:, :]), high, True)
    top = slice(half + PAD, None)
    inner_ref[top, :] = first
    outer_ref[top, :] = first
    pack_grams(inner_ref, [jnp.where(even, b, a) for a, b in zip(lows, highs)], below, diagonal)
    pack_grams(outer_ref, [jnp.where(even, a, b) for a, b in zip(lows, highs)], below, diagonal)


def local_kernel(layout, width, half, index_ref, *refs):
    count = len(layout)
    pieces = [(refs[at], layout[at]) for at in range(count)]
    (
        matrix_ref, straddle_ref, inner_ref, inner_got_ref, outer_ref, outer_got_ref,
        wide_ref, step_ref, up_ref, state_ref, seen_ref, square_ref, factor_ref,
    ) = refs[count:]
    place(pieces, index_ref, 4, wide_ref, width)
    parity = index_ref[0]
    even = parity == 0
    outside = jnp.where(index_ref[1] == 0, 1.0, 0.0)
    columns = matrix_ref.shape[1]
    below, diagonal = triangle(half)
    blank = jnp.zeros((half, half), F32)
    low_lanes, high_lanes = slice(0, half), slice(half, None)

    current = jnp.transpose(matrix_ref[...])
    whole = split(current)
    upper, lower = cut(whole, lanes=low_lanes), cut(whole, lanes=high_lanes)
    straddle = [split(straddle_ref[sweep]) for sweep in range(2)]
    aligned = [split(wide_ref[sweep]) for sweep in range(2)]
    bottom = [cut(value, lanes=low_lanes) for value in straddle]
    top = [cut(value, lanes=high_lanes) for value in straddle]
    first = [cut(value, lanes=low_lanes) for value in aligned]
    last = [cut(value, lanes=high_lanes) for value in aligned]

    inner = inner_ref[0 : half + PAD, :] + inner_got_ref[0 : half + PAD, :]
    outer = outer_ref[0 : half + PAD, :] + outside * outer_got_ref[0 : half + PAD, :]
    stricts, diagonals = [], []
    for packed in (inner, outer):
        mixed = packed[0:half]
        stricts.append(jnp.where(below, mixed, 0.0))
        stricts.append(jnp.where(below, jnp.transpose(mixed), 0.0))
        diagonals.append(packed[half : half + 1])
        diagonals.append(packed[half + 1 : half + 2])
    for value in aligned:
        gram = product(value, value, True)
        stricts.append(jnp.where(below, gram, 0.0))
        diagonals.append(jnp.sum(jnp.where(diagonal, gram, 0.0), axis=0, keepdims=True))
    factors = lower_inverses(stricts, diagonals)

    through = [product(t, a, True) for t, a in zip(top, last)]
    onward = [product(a, b, True) for a, b in zip(first, bottom)]
    seen0, seen1 = (product(whole, value, True) for value in aligned)
    raw0, raw1 = (product(upper, value, True) for value in bottom)
    second = product(lower, top[1], True)
    cross_aligned = split(product(aligned[0], aligned[1], True))
    cross_bottom_aligned = split(product(bottom[0], first[1], True))
    cross_top_aligned = split(product(top[0], last[1], True))
    cross_top = split(product(top[0], top[1], True))
    cross_aligned_top = split(product(last[0], top[1], True))
    cross_aligned_bottom = split(product(first[0], bottom[1], True))
    cross_bottom = split(product(bottom[0], bottom[1], True))

    for sweep in range(2):
        square_ref[sweep, parity] = factors[sweep]
        square_ref[sweep, 1 - parity] = factors[2 + sweep]
    factor_top = [split(square_ref[sweep, 0]) for sweep in range(2)]
    factor_bottom = split(square_ref[0, 1])
    factor_aligned = [split(value) for value in factors[4:]]
    rows = slice(half + PAD, None)
    own_first = inner_ref[rows, :]
    got_first = jnp.where(even, outside * outer_got_ref[rows, :], inner_got_ref[rows, :])

    reached = [product(f, value) for f, value in zip(factor_top, through)]
    leaving = [product(f, value) for f, value in zip(factor_aligned, onward)]
    reached_pair = [split(value) for value in reached]
    leaving_pair = [split(value) for value in leaving]
    own_pair = split(own_first)
    step1 = product(reached_pair[1], leaving_pair[1])
    outer_coeff = stack(product(own_pair, factor_top[0]), square_ref[0, 0])
    inside = split(stack(seen0 - product(own_pair, reached_pair[0]), -reached[0]))
    carry0 = stack(raw0, blank) - product(inside, leaving_pair[0])
    coeffs = product(inside, factor_aligned[0])
    back = product(stack(carry0[:columns] + got_first, carry0[columns:]), factor_bottom)
    outer_pair, coeff_pair, back_pair = split(outer_coeff), split(coeffs), split(back)
    begun = (
        stack(second, blank)
        - product(outer_pair, cross_top)
        - product(coeff_pair, cross_aligned_top)
    )
    seen = (
        stack(seen1, blank)
        - product(coeff_pair, cross_aligned)
        - product(outer_pair, cross_top_aligned)
        - product(back_pair, cross_bottom_aligned)
    )
    raw = (
        stack(raw1, blank)
        - product(coeff_pair, cross_aligned_bottom)
        - product(back_pair, cross_bottom)
    )
    carry1 = raw - product(seen, leaving_pair[1]) + product(begun, step1)
    up_ref[...] = begun
    seen_ref[...] = seen
    state_ref[:, 0:half] = outer_coeff
    state_ref[:, half : 2 * half] = coeffs
    state_ref[:, 2 * half :] = back
    factor_ref[0] = square_ref[1, 0]
    factor_ref[1] = square_ref[1, 1]
    factor_ref[2] = factors[5]
    factor_ref[3] = reached[1]
    step_ref[0:half, :] = carry0[columns:]
    step_ref[half : 2 * half, :] = carry1[columns:]
    step_ref[2 * half : 3 * half, :] = step1
    step_ref[3 * half : 3 * half + columns, :] = carry0[:columns]
    step_ref[3 * half + columns :, :] = carry1[:columns]


def by_core(index_ref, body, own_ref, got_ref):
    @pl.when(index_ref[0] == 0)
    def _():
        body(own_ref, got_ref)

    @pl.when(index_ref[0] != 0)
    def _():
        body(got_ref, own_ref)


def compose_kernel(half, index_ref, own_ref, got_ref, high_ref, low_ref, start_ref):
    part = start_ref.shape[0]

    def store(at, value):
        high, low = split(value)
        high_ref[at * half : (at + 1) * half, :] = high
        low_ref[at * half : (at + 1) * half, :] = low

    def body(even_ref, odd_ref):
        even0, even_mix, even1 = (
            split(even_ref[at * half : (at + 1) * half, :]) for at in range(3)
        )
        odd0, odd_mix, odd1 = (split(odd_ref[at * half : (at + 1) * half, :]) for at in range(3))

        def rows(ref, sweep):
            first = pl.multiple_of(3 * half + 2 * sweep * part + index_ref[0] * part, 8)
            return ref[pl.ds(first, part), :]

        odd_first = split(rows(odd_ref, 0))
        start_ref[:, :half] = rows(even_ref, 0) + product(odd_first, even0)
        start_ref[:, half:] = (
            rows(even_ref, 1) + product(odd_first, even_mix) + product(rows(odd_ref, 1), even1)
        )
        store(0, product(odd0, even0))
        store(1, product(odd0, even_mix) + product(odd_mix, even1))
        store(2, product(odd1, even1))

    by_core(index_ref, body, own_ref, got_ref)


def hop_kernel(half, start_ref, high_ref, low_ref, got_ref, after_ref, out_ref):
    zero, one = split(got_ref[:, :half]), split(got_ref[:, half:])

    def chain(at):
        rows = slice(at * half, (at + 1) * half)
        return high_ref[rows, :], low_ref[rows, :]

    out_ref[:, :half] = start_ref[:, :half] + product(zero, chain(0))
    out_ref[:, half:] = (
        start_ref[:, half:] + product(zero, chain(1)) + product(one, chain(2))
    )


def sweep_kernel(
    half, matrix_ref, up_ref, state_ref, seen_ref, factor_ref, straddle_ref, wide_ref, out_ref
):
    columns = matrix_ref.shape[1]
    reach = columns + half
    low_lanes, high_lanes = slice(0, half), slice(half, None)
    outer = split(state_ref[:, 0:half])
    coeffs = split(state_ref[:, half : 2 * half])
    back = split(state_ref[:, 2 * half :])
    begun = split(up_ref[...])
    reached = factor_ref[3]
    inside = stack(seen_ref[...] - product(begun, reached), -reached)
    next_outer = split(stack(product(begun, factor_ref[0]), factor_ref[0]))
    next_coeffs = split(product(inside, factor_ref[2]))
    current = jnp.transpose(matrix_ref[...])
    straddle, aligned = split(straddle_ref[0]), split(wide_ref[0])
    change = beside(
        product(coeffs, cut(aligned, lanes=low_lanes))
        + product(back, cut(straddle, lanes=low_lanes)),
        product(outer, cut(straddle, lanes=high_lanes))
        + product(coeffs, cut(aligned, lanes=high_lanes)),
    )
    straddle, aligned = split(straddle_ref[1]), split(wide_ref[1])
    later = beside(
        product(next_coeffs, cut(aligned, lanes=low_lanes)),
        product(next_outer, cut(straddle, lanes=high_lanes))
        + product(next_coeffs, cut(aligned, lanes=high_lanes)),
    )
    out_ref[:columns, :] = current - change[:columns] - later[:columns]
    out_ref[columns:reach, :] = -change[columns:] - later[columns:reach]
    out_ref[reach:, :] = -later[reach:]


def response_kernel(
    half, index_ref, own_ref, got_ref, up_ref, local_ref, factor_ref, straddle_ref,
    base_ref, high_ref, low_ref,
):
    columns = base_ref.shape[0]
    reach = columns + half
    keep = jnp.where(index_ref[2] == 0, 1.0, 0.0)
    first_rows = slice(3 * half, 3 * half + columns)
    first = stack(own_ref[first_rows, :], own_ref[0:half, :])
    offset = product(first, keep * up_ref[columns:, :])
    summed = stack(
        own_ref[3 * half + columns :, :] + offset[:columns] + keep * up_ref[:columns, :],
        own_ref[half : 2 * half, :] + offset[columns:],
        own_ref[2 * half : 3 * half, :],
    )
    back = product(summed, factor_ref[1])
    change = product(back, straddle_ref[1][:, :half])
    local = beside(local_ref[:, :half] - change, local_ref[:, half:])
    base, middle, last = local[:columns], local[columns:reach], local[reach:]

    def store(at, value):
        high, low = split(value)
        high_ref[at * half : (at + 1) * half, :] = high
        low_ref[at * half : (at + 1) * half, :] = low

    @pl.when(index_ref[0] != 0)
    def _():
        base_ref[...] = base
        store(0, middle)
        store(1, last)

    @pl.when(index_ref[0] == 0)
    def _():
        middle_pair, last_pair = split(middle), split(last)
        zero = stack(got_ref[first_rows, :], got_ref[0:half, :])
        one = stack(got_ref[3 * half + columns :, :], got_ref[half : 3 * half, :])
        after_zero = product(zero, middle_pair)
        after_one = product(one, last_pair)
        base_ref[...] = base + after_zero[:columns] + after_one[:columns]
        store(0, after_zero[columns:] + after_one[columns:reach])
        store(1, after_one[reach:])


def final_kernel(index_ref, own_ref, got_ref, base_ref, high_ref, low_ref, out_ref):
    def body(even_ref, odd_ref):
        carry = stack(even_ref[...], odd_ref[...])
        reply = high_ref[...], low_ref[...]
        out_ref[...] = jnp.transpose(base_ref[...] + product(carry, reply))

    by_core(index_ref, body, own_ref, got_ref)


def call(body, outs, *operands, flops=0, free=()):
    space = pl.BlockSpec(memory_space=pltpu.VMEM)
    specs = []
    for at, operand in enumerate(operands):
        if operand.dtype == jnp.int32:
            specs.append(pl.BlockSpec(memory_space=pltpu.SMEM))
        else:
            specs.append(pl.BlockSpec(memory_space=pl.ANY) if at in free else space)
    shapes = [
        shape if isinstance(shape, jax.ShapeDtypeStruct) else jax.ShapeDtypeStruct(shape, F32)
        for shape in outs
    ]
    moved = sum(4 * operand.size for operand in operands) + sum(4 * shape.size for shape in shapes)
    return pl.pallas_call(
        body,
        out_shape=shapes,
        in_specs=specs,
        out_specs=[space] * len(shapes),
        compiler_params=pltpu.CompilerParams(vmem_limit_bytes=VMEM_GRANT),
        cost_estimate=pl.CostEstimate(flops=flops, bytes_accessed=moved, transcendentals=0),
    )(*operands)


def gathered(shard, axis):
    count = lax.axis_size(axis)
    me = lax.axis_index(axis)
    every = ((0, 0), (1, 1))
    power = count & (count - 1) == 0
    arrays, places, layout = [shard], [me], [every]
    for step in range(1, count):
        route = [(i ^ step if power else (i + step) % count, i) for i in range(count)]
        arrays.append(lax.ppermute(shard, axis, route))
        places.append(me ^ step if power else (me + step) % count)
        layout.append(every)
    return arrays, places, layout


def on_device(eigenvectors, aligned_vectors, straddle_vectors):
    aligned = jnp.swapaxes(aligned_vectors, 1, 2)
    straddle = jnp.swapaxes(straddle_vectors, 1, 2)
    sweeps, width, span = aligned.shape
    half = span // 2
    columns = eigenvectors.shape[1]
    part = columns // 2
    rows = lax.axis_size("row")
    row = lax.axis_index("row")
    chips = rows // 2

    straddle_parts, places, layout = gathered(straddle, "col")
    aligned_parts, _, _ = gathered(aligned, "col")
    parity = row % 2
    outside = jnp.where(parity == 0, row == 0, row == rows - 1)
    index = jnp.stack(
        [parity, outside.astype(jnp.int32), (row == 0).astype(jnp.int32), row]
        + [jnp.asarray(place, jnp.int32) for place in places]
    ).astype(jnp.int32)
    unit = 2 * half * half * half * 3
    message = (half + PAD + columns, half)
    reach = columns + half

    wide_straddle, inner, outer = call(
        functools.partial(gram_kernel, layout, width, half),
        [(sweeps, half, span), message, message],
        index, *straddle_parts, eigenvectors, flops=5 * unit,
    )
    inside_route = [(i, i ^ 1) for i in range(rows)]
    outside_route = [(i, (i - 1 if i % 2 == 0 else i + 1) % rows) for i in range(rows)]
    outer_got = lax.ppermute(outer, "row", outside_route)
    inner_got = lax.ppermute(inner, "row", inside_route)
    wide_aligned, step, up, state, seen, _, factor = call(
        functools.partial(local_kernel, layout, width, half),
        [
            (sweeps, half, span), (3 * half + 2 * columns, half), (reach, half), (reach, 3 * half),
            (reach, half), (2, 2, half, half), (4, half, half),
        ],
        index, *aligned_parts, eigenvectors, wide_straddle, inner, inner_got, outer, outer_got,
        flops=100 * unit,
    )
    step_got = lax.ppermute(step, "row", inside_route)
    up_got = lax.ppermute(up, "row", [(i, i + 1) for i in range(rows - 1)])
    halves = jax.ShapeDtypeStruct((3 * half, half), BF16)
    high, low, start = call(
        functools.partial(compose_kernel, half),
        [halves, halves, (part, span)],
        index, step, step_got, flops=6 * unit,
    )
    down = [(i, i - 2) for i in range(2, rows)]
    local = base = None

    def shadow(local, base):
        if local is None:
            (local,) = call(
                functools.partial(sweep_kernel, half), [(reach + half, span)],
                eigenvectors, up, state, seen, factor, wide_straddle, wide_aligned,
                flops=20 * unit,
            )
            return local, None, (), local
        wide_halves = jax.ShapeDtypeStruct((span, span), BF16)
        base, *reply = call(
            functools.partial(response_kernel, half),
            [(columns, span), wide_halves, wide_halves],
            index, step, step_got, up_got, local, factor, wide_straddle, flops=20 * unit,
        )
        return local, base, reply, base

    carry, reply, got = start, (), jnp.zeros_like(start)
    for hop in range(chips - 1):
        got = lax.ppermute(carry, "row", down)
        after = start
        if base is None:
            local, base, reply, after = shadow(local, base)
        if hop < chips - 2:
            (carry,) = call(
                functools.partial(hop_kernel, half), [(part, span)],
                start, high, low, got, after, flops=unit, free=(4,),
            )
    while base is None:
        local, base, reply, after = shadow(local, base)
    other = lax.ppermute(got, "row", inside_route)
    (result,) = call(
        final_kernel, [(span, columns)], index, got, other, base, *reply, flops=4 * unit
    )
    return result


def solution(mesh):
    placed = (P("row", "col"), P(None, "row", "col"), P(None, "row", "col"))

    return jax.shard_map(
        on_device, mesh=mesh, in_specs=placed, out_specs=P("row", "col"), check_vma=False
    )
```

```python
import functools

import jax
import jax.numpy as jnp
from jax import lax
from jax.experimental import pallas as pl
from jax.experimental.pallas import tpu as pltpu
from jax.sharding import PartitionSpec as P


F32 = jnp.float32
BF16 = jnp.bfloat16
BASE_BLOCK = 32
LANES = 128
PAD = 8
VMEM_GRANT = 16 * 1024 * 1024


def split(value):
    high = value.astype(BF16)
    return high, (value - high.astype(F32)).astype(BF16)


def raw_dot(left, right, transposed):
    dims = (((1,), (1 if transposed else 0,)), ((), ()))
    return lax.dot_general(left, right, dims, preferred_element_type=F32)


def product(left, right, transposed=False):
    left = left if isinstance(left, tuple) else split(left)
    right = right if isinstance(right, tuple) else split(right)
    return (
        raw_dot(left[0], right[0], transposed)
        + raw_dot(left[0], right[1], transposed)
        + raw_dot(left[1], right[0], transposed)
    )


def cut(pair, rows=slice(None), lanes=slice(None)):
    return pair[0][rows, lanes], pair[1][rows, lanes]


def stack(*values):
    return jnp.concatenate(values, axis=0)


def beside(*values):
    return jnp.concatenate(values, axis=1)


def block_inverse(packed, base):
    done = []
    for start in range(0, packed.shape[1], LANES):
        entries = packed[:, start : start + LANES]
        rows = lax.broadcasted_iota(jnp.int32, entries.shape, 0)
        lanes = lax.broadcasted_iota(jnp.int32, entries.shape, 1)
        group = (lanes // base) * base
        value = jnp.where(rows == lanes - group, 1.0, 0.0).astype(F32)
        for step in range(base - 1):
            top = (step // 8) * 8
            factor = jnp.take_along_axis(entries[top:], (group + step)[top:], axis=1)
            changed = value[top:] - factor * value[step : step + 1]
            value = stack(value[:top], changed) if top else changed
        done.append(value)
    return beside(*done)


def small_inverse(strict, across, base):
    order = strict.shape[0]
    lanes = lax.broadcasted_iota(jnp.int32, (base, order), 1) // base
    packed = jnp.zeros((base, order), F32)
    for block in range(order // base):
        packed = jnp.where(lanes == block, strict[block * base : (block + 1) * base], packed)
    solved = block_inverse(packed * across, base)
    return stack(*[jnp.where(lanes == block, solved, 0.0) for block in range(order // base)])


def lower_inverses(stricts, diagonals):
    order = stricts[0].shape[0]
    base = min(BASE_BLOCK, order)
    rows = lax.broadcasted_iota(jnp.int32, (order, order), 0)
    lanes = lax.broadcasted_iota(jnp.int32, (order, order), 1)
    result = []
    for strict, diagonal in zip(stricts, diagonals):
        across = 2.0 / diagonal
        along = jnp.sum(jnp.where(rows == lanes, across, 0.0), axis=1, keepdims=True)
        result.append(small_inverse(strict, across, base) * along)
    size = base
    while 2 * size < order:
        here = (rows // (2 * size) == lanes // (2 * size)) & (rows // size != lanes // size)
        wholes = [split(now) for now in result]
        starts = range(0, order, 2 * size)
        odds = [
            tuple(stack(*[part[at + size : at + 2 * size] for at in starts]) for part in whole)
            for whole in wholes
        ]
        inner = [
            product(odd, jnp.where(here, strict, 0.0)) for odd, strict in zip(odds, stricts)
        ]
        outer = [product(value, whole) for value, whole in zip(inner, wholes)]
        merged = []
        for now, change in zip(result, outer):
            bands = []
            for number, at in enumerate(starts):
                bands.append(now[at : at + size])
                bands.append(
                    now[at + size : at + 2 * size] - change[number * size : (number + 1) * size]
                )
            merged.append(stack(*bands))
        result = merged
        size *= 2
    if size < order:
        wholes = [split(now) for now in result]
        low, high = slice(0, size), slice(size, None)
        inner = [
            product(cut(whole, high, high), strict[high, low])
            for whole, strict in zip(wholes, stricts)
        ]
        outer = [product(value, cut(whole, low, low)) for value, whole in zip(inner, wholes)]
        result = [
            stack(now[low], beside(-change, now[high, high]))
            for now, change in zip(result, outer)
        ]
    return result


def core_now():
    return lax.axis_index("row") % 2


def chip_now():
    return lax.axis_index("row") // 2


def source_place(count, step):
    me = lax.axis_index("col")
    return me ^ step if count & (count - 1) == 0 else (me + step) % count


def place(layout, count, pieces, target):
    for (step, sweep), piece in zip(layout, pieces):
        width = piece.shape[1]
        start = pl.multiple_of(source_place(count, step) * width, width)
        for at in range(piece.shape[0]):
            target[sweep + at, pl.ds(start, width), :] = piece[at]


def triangle(order):
    rows = lax.broadcasted_iota(jnp.int32, (order, order), 0)
    lanes = lax.broadcasted_iota(jnp.int32, (order, order), 1)
    return rows > lanes, rows == lanes


def pack_grams(target, pair, below, diagonal):
    half = pair[0].shape[0]
    target[0:half, :] = jnp.where(below, pair[0], pair[1])
    for at, gram in enumerate(pair):
        target[half + at : half + at + 1, :] = jnp.sum(
            jnp.where(diagonal, gram, 0.0), axis=0, keepdims=True
        )


def first_kernel(matrix_ref, straddle_ref, aligned_ref, current_ref, own_ref, early_ref, late_ref):
    current_ref[...] = jnp.transpose(matrix_ref[...])
    own_ref[...] = straddle_ref[...]
    early_ref[...] = aligned_ref[0:1]
    late_ref[...] = aligned_ref[1:2]


def gram_kernel(layout, count, half, *refs):
    current_ref, wide_ref, inner_ref, outer_ref = refs[len(layout) :]
    place(layout, count, refs[: len(layout)], wide_ref)
    even = core_now() == 0
    below, diagonal = triangle(half)
    lows, highs = [], []
    for sweep in range(2):
        whole = split(wide_ref[sweep])
        low, high = cut(whole, lanes=slice(0, half)), cut(whole, lanes=slice(half, None))
        lows.append(product(low, low, True))
        highs.append(product(high, high, True))
        if sweep == 0:
            first = product(current_ref[:, half:], high, True)
    top = slice(half + PAD, None)
    inner_ref[top, :] = first
    outer_ref[top, :] = first
    pack_grams(inner_ref, [jnp.where(even, b, a) for a, b in zip(lows, highs)], below, diagonal)
    pack_grams(outer_ref, [jnp.where(even, a, b) for a, b in zip(lows, highs)], below, diagonal)


def keep_pairs(high_ref, low_ref, values):
    for at, value in enumerate(values):
        high_ref[at], low_ref[at] = split(value)


def between_kernel(half, current_ref, straddle_ref, high_ref, low_ref, raw_ref):
    whole = split(current_ref[...])
    upper, lower = cut(whole, lanes=slice(0, half)), cut(whole, lanes=slice(half, None))
    straddle = [split(straddle_ref[sweep]) for sweep in range(2)]
    bottom = [cut(value, lanes=slice(0, half)) for value in straddle]
    top = [cut(value, lanes=slice(half, None)) for value in straddle]
    keep_pairs(
        high_ref, low_ref, [product(top[0], top[1], True), product(bottom[0], bottom[1], True)]
    )
    raw_ref[0] = product(upper, bottom[0], True)
    raw_ref[1] = product(upper, bottom[1], True)
    raw_ref[2] = product(lower, top[1], True)


def aligned_kernel(layout, count, half, *refs):
    current_ref, straddle_ref, wide_ref, high_ref, low_ref, seen_ref = refs[len(layout) :]
    place(layout, count, refs[: len(layout)], wide_ref)
    below, diagonal = triangle(half)
    low_lanes, high_lanes = slice(0, half), slice(half, None)
    aligned = [split(wide_ref[sweep]) for sweep in range(2)]
    straddle = [split(straddle_ref[sweep]) for sweep in range(2)]
    bottom = [cut(value, lanes=low_lanes) for value in straddle]
    top = [cut(value, lanes=high_lanes) for value in straddle]
    first = [cut(value, lanes=low_lanes) for value in aligned]
    last = [cut(value, lanes=high_lanes) for value in aligned]
    grams = [product(value, value, True) for value in aligned]
    factors = lower_inverses(
        [jnp.where(below, gram, 0.0) for gram in grams],
        [jnp.sum(jnp.where(diagonal, gram, 0.0), axis=0, keepdims=True) for gram in grams],
    )
    whole = split(current_ref[...])
    seen_ref[0] = product(whole, aligned[0], True)
    seen_ref[1] = product(whole, aligned[1], True)
    through = [product(t, a, True) for t, a in zip(top, last)]
    onward = [product(a, b, True) for a, b in zip(first, bottom)]
    crosses = [
        product(aligned[0], aligned[1], True),
        product(bottom[0], first[1], True),
        product(top[0], last[1], True),
        product(last[0], top[1], True),
        product(first[0], bottom[1], True),
    ]
    leaving = [product(f, value) for f, value in zip(factors, onward)]
    keep_pairs(high_ref, low_ref, factors + leaving + through + crosses)


def local_kernel(
    columns, half, inner_ref, inner_got_ref, outer_ref, outer_got_ref,
    high_ref, low_ref, seen_ref, straddle_high_ref, straddle_low_ref, raw_ref,
    step_ref, up_ref, state_ref, sight_ref, factor_ref, square_ref,
):
    parity = core_now()
    below, _ = triangle(half)
    blank = jnp.zeros((half, half), F32)
    inner = inner_ref[0 : half + PAD, :] + inner_got_ref[0 : half + PAD, :]
    outer = outer_ref[0 : half + PAD, :] + outer_got_ref[0 : half + PAD, :]
    stricts, diagonals = [], []
    for packed in (inner, outer):
        mixed = packed[0:half]
        stricts.append(jnp.where(below, mixed, 0.0))
        stricts.append(jnp.where(below, jnp.transpose(mixed), 0.0))
        diagonals.append(packed[half : half + 1])
        diagonals.append(packed[half + 1 : half + 2])
    factors = lower_inverses(stricts, diagonals)

    def held(at):
        return high_ref[at], low_ref[at]

    factor_aligned, leaving, through = held(0), [held(2), held(3)], [held(4), held(5)]
    cross_aligned, cross_bottom_aligned, cross_top_aligned = held(6), held(7), held(8)
    cross_aligned_top, cross_aligned_bottom = held(9), held(10)
    cross_top = straddle_high_ref[0], straddle_low_ref[0]
    cross_bottom = straddle_high_ref[1], straddle_low_ref[1]
    for sweep in range(2):
        square_ref[sweep, parity] = factors[sweep]
        square_ref[sweep, 1 - parity] = factors[2 + sweep]
    factor_top = [split(square_ref[sweep, 0]) for sweep in range(2)]
    factor_bottom = split(square_ref[0, 1])
    rows = slice(half + PAD, None)
    own_first = inner_ref[rows, :]
    got_first = jnp.where(parity == 0, outer_got_ref[rows, :], inner_got_ref[rows, :])

    reached = [product(f, value) for f, value in zip(factor_top, through)]
    reached_pair = [split(value) for value in reached]
    own_pair = split(own_first)
    step1 = product(reached_pair[1], leaving[1])
    outer_coeff = stack(product(own_pair, factor_top[0]), square_ref[0, 0])
    inside = split(stack(seen_ref[0] - product(own_pair, reached_pair[0]), -reached[0]))
    carry0 = stack(raw_ref[0], blank) - product(inside, leaving[0])
    coeffs = product(inside, factor_aligned)
    back = product(stack(carry0[:columns] + got_first, carry0[columns:]), factor_bottom)
    outer_pair, coeff_pair, back_pair = split(outer_coeff), split(coeffs), split(back)
    begun = (
        stack(raw_ref[2], blank)
        - product(outer_pair, cross_top)
        - product(coeff_pair, cross_aligned_top)
    )
    sight = (
        stack(seen_ref[1], blank)
        - product(coeff_pair, cross_aligned)
        - product(outer_pair, cross_top_aligned)
        - product(back_pair, cross_bottom_aligned)
    )
    raw = (
        stack(raw_ref[1], blank)
        - product(coeff_pair, cross_aligned_bottom)
        - product(back_pair, cross_bottom)
    )
    carry1 = raw - product(sight, leaving[1]) + product(begun, step1)
    up_ref[...] = begun
    sight_ref[...] = sight
    state_ref[:, 0:half] = outer_coeff
    state_ref[:, half : 2 * half] = coeffs
    state_ref[:, 2 * half :] = back
    factor_ref[0] = square_ref[1, 0]
    factor_ref[1] = square_ref[1, 1]
    factor_ref[2] = reached[1]
    step_ref[0:half, :] = carry0[columns:]
    step_ref[half : 2 * half, :] = carry1[columns:]
    step_ref[2 * half : 3 * half, :] = step1
    step_ref[3 * half : 3 * half + columns, :] = carry0[:columns]
    step_ref[3 * half + columns :, :] = carry1[:columns]


def by_core(body, own_ref, got_ref):
    @pl.when(core_now() == 0)
    def _():
        body(own_ref, got_ref)

    @pl.when(core_now() != 0)
    def _():
        body(got_ref, own_ref)


def chain_parts(ref, half):
    return [split(ref[at * half : (at + 1) * half, :]) for at in range(3)]


def start_kernel(half, own_ref, got_ref, start_ref):
    part = start_ref.shape[0]

    def body(even_ref, odd_ref):
        even0, even_mix, even1 = chain_parts(even_ref, half)

        def rows(ref, sweep):
            first = pl.multiple_of(3 * half + 2 * sweep * part + core_now() * part, 8)
            return ref[pl.ds(first, part), :]

        odd_first = split(rows(odd_ref, 0))
        start_ref[:, :half] = rows(even_ref, 0) + product(odd_first, even0)
        start_ref[:, half:] = (
            rows(even_ref, 1) + product(odd_first, even_mix) + product(rows(odd_ref, 1), even1)
        )

    by_core(body, own_ref, got_ref)


def chain_kernel(half, own_ref, got_ref, high_ref, low_ref):
    def body(even_ref, odd_ref):
        even0, even_mix, even1 = chain_parts(even_ref, half)
        odd0, odd_mix, odd1 = chain_parts(odd_ref, half)
        keep_pairs(
            high_ref,
            low_ref,
            [
                product(odd0, even0),
                product(odd0, even_mix) + product(odd_mix, even1),
                product(odd1, even1),
            ],
        )

    by_core(body, own_ref, got_ref)


def hop_kernel(
    half, receiver, start_ref, high_ref, low_ref, got_ref, kept_ref, out_ref, keep_ref
):
    got = got_ref[...]
    zero, one = split(got[:, :half]), split(got[:, half:])

    def chain(at):
        return high_ref[at], low_ref[at]

    out_ref[:, :half] = start_ref[:, :half] + product(zero, chain(0))
    out_ref[:, half:] = (
        start_ref[:, half:] + product(zero, chain(1)) + product(one, chain(2))
    )
    keep_ref[...] = jnp.where(chip_now() == receiver, got, kept_ref[...])


def sweep_kernel(
    half, current_ref, up_ref, state_ref, sight_ref, factor_ref, high_ref, low_ref,
    straddle_ref, wide_ref, out_ref,
):
    columns = current_ref.shape[0]
    reach = columns + half
    low_lanes, high_lanes = slice(0, half), slice(half, None)
    outer = split(state_ref[:, 0:half])
    coeffs = split(state_ref[:, half : 2 * half])
    back = split(state_ref[:, 2 * half :])
    begun = split(up_ref[...])
    reached = factor_ref[2]
    inside = stack(sight_ref[...] - product(begun, reached), -reached)
    next_outer = split(stack(product(begun, factor_ref[0]), factor_ref[0]))
    next_coeffs = split(product(inside, (high_ref[1], low_ref[1])))
    current = current_ref[...]
    straddle, aligned = split(straddle_ref[0]), split(wide_ref[0])
    change = beside(
        product(coeffs, cut(aligned, lanes=low_lanes))
        + product(back, cut(straddle, lanes=low_lanes)),
        product(outer, cut(straddle, lanes=high_lanes))
        + product(coeffs, cut(aligned, lanes=high_lanes)),
    )
    straddle, aligned = split(straddle_ref[1]), split(wide_ref[1])
    later = beside(
        product(next_coeffs, cut(aligned, lanes=low_lanes)),
        product(next_outer, cut(straddle, lanes=high_lanes))
        + product(next_coeffs, cut(aligned, lanes=high_lanes)),
    )
    out_ref[:columns, :] = current - change[:columns] - later[:columns]
    out_ref[columns:reach, :] = -change[columns:] - later[columns:reach]
    out_ref[reach:, :] = -later[reach:]


def response_kernel(
    half, own_ref, got_ref, up_ref, local_ref, factor_ref, straddle_ref,
    base_ref, high_ref, low_ref,
):
    columns = base_ref.shape[0]
    reach = columns + half
    first_rows = slice(3 * half, 3 * half + columns)
    first = stack(own_ref[first_rows, :], own_ref[0:half, :])
    offset = product(first, up_ref[columns:, :])
    summed = stack(
        own_ref[3 * half + columns :, :] + offset[:columns] + up_ref[:columns, :],
        own_ref[half : 2 * half, :] + offset[columns:],
        own_ref[2 * half : 3 * half, :],
    )
    back = product(summed, factor_ref[1])
    change = product(back, straddle_ref[1][:, :half])
    local = beside(local_ref[:, :half] - change, local_ref[:, half:])
    base, middle, last = local[:columns], local[columns:reach], local[reach:]

    def store(at, value):
        high, low = split(value)
        high_ref[at * half : (at + 1) * half, :] = high
        low_ref[at * half : (at + 1) * half, :] = low

    @pl.when(core_now() != 0)
    def _():
        base_ref[...] = base
        store(0, middle)
        store(1, last)

    @pl.when(core_now() == 0)
    def _():
        middle_pair, last_pair = split(middle), split(last)
        zero = stack(got_ref[first_rows, :], got_ref[0:half, :])
        one = stack(got_ref[3 * half + columns :, :], got_ref[half : 3 * half, :])
        after_zero = product(zero, middle_pair)
        after_one = product(one, last_pair)
        base_ref[...] = base + after_zero[:columns] + after_one[:columns]
        store(0, after_zero[columns:] + after_one[columns:reach])
        store(1, after_one[reach:])


def final_kernel(
    own_ref, got_ref, own_kept_ref, got_kept_ref, base_ref, high_ref, low_ref, out_ref
):
    last = chip_now() == 0

    def body(even_ref, odd_ref, even_kept_ref, odd_kept_ref):
        carry = jnp.where(
            last,
            stack(even_ref[...], odd_ref[...]),
            stack(even_kept_ref[...], odd_kept_ref[...]),
        )
        reply = high_ref[...], low_ref[...]
        out_ref[...] = jnp.transpose(base_ref[...] + product(carry, reply))

    @pl.when(core_now() == 0)
    def _():
        body(own_ref, got_ref, own_kept_ref, got_kept_ref)

    @pl.when(core_now() != 0)
    def _():
        body(got_ref, own_ref, got_kept_ref, own_kept_ref)


def call(body, outs, *operands, flops=0):
    space = pl.BlockSpec(memory_space=pltpu.VMEM)
    shapes = [
        shape if isinstance(shape, jax.ShapeDtypeStruct) else jax.ShapeDtypeStruct(shape, F32)
        for shape in outs
    ]
    moved = sum(4 * operand.size for operand in operands) + sum(4 * shape.size for shape in shapes)
    return pl.pallas_call(
        body,
        out_shape=shapes,
        in_specs=[space] * len(operands),
        out_specs=[space] * len(shapes),
        compiler_params=pltpu.CompilerParams(vmem_limit_bytes=VMEM_GRANT),
        cost_estimate=pl.CostEstimate(flops=flops, bytes_accessed=moved, transcendentals=0),
    )(*operands)


def swap_route(count, step):
    power = count & (count - 1) == 0
    return [(i ^ step if power else (i + step) % count, i) for i in range(count)]


def passed(value, step):
    count = lax.axis_size("col")
    return lax.ppermute(value, "col", swap_route(count, step))


def gathered(straddle, own, early, late):
    count = lax.axis_size("col")
    if count == 4:
        near, side = passed(straddle, 1), passed(straddle, 2)
        near_late, side_early = passed(late, 1), passed(early, 2)
        far_early, far_late = passed(side[0:1], 1), passed(near[1:2], 2)
        near_early, side_late = passed(early, 1), passed(late, 2)
        first = [own, near, side, far_early, far_late]
        first_layout = [(0, 0), (1, 0), (2, 0), (3, 0), (3, 1)]
        second = [early, late, near_early, near_late, side_early, side_late]
        second += [passed(side_early, 1), passed(near_late, 2)]
        second_layout = [(step, sweep) for step in range(4) for sweep in range(2)]
        return first, first_layout, second, second_layout
    steps = range(1, count)
    first = [own] + [passed(straddle, step) for step in steps]
    second, second_layout = [early, late], [(0, 0), (0, 1)]
    for step in steps:
        for sweep, value in enumerate((early, late)):
            second.append(passed(value, step))
            second_layout.append((step, sweep))
    return first, [(step, 0) for step in range(count)], second, second_layout


def hop_routes(chips):
    routes = []
    for round_at in range(1, chips):
        pairs = {}
        for chip in range(chips - 2 + round_at % 2, 0, -2):
            pairs[chip], pairs[chip - 1] = chip - 1, chip
        route = []
        for chip in range(chips):
            for core in range(2):
                route.append((2 * chip + core, 2 * pairs[chip] + core if chip in pairs else 2 * chip + 1 - core))
        routes.append(route)
    return routes


def on_device(eigenvectors, aligned_vectors, straddle_vectors):
    aligned = jnp.swapaxes(aligned_vectors, 1, 2)
    straddle = jnp.swapaxes(straddle_vectors, 1, 2)
    sweeps, width, span = aligned.shape
    half = span // 2
    columns = eigenvectors.shape[1]
    part = columns // 2
    rows = lax.axis_size("row")
    chips = rows // 2
    unit = 2 * half * half * half * 3
    message = (half + PAD + columns, half)
    reach = columns + half
    half_pairs = lambda count: [jax.ShapeDtypeStruct((count, half, half), BF16)] * 2

    count = lax.axis_size("col")
    shard = (sweeps, width, span)
    current, own, early, late = call(
        first_kernel, [(columns, span), shard, (1,) + shard[1:], (1,) + shard[1:]],
        eigenvectors, straddle, aligned,
    )
    first, first_layout, second, second_layout = gathered(straddle, own, early, late)
    wide_straddle, inner, outer = call(
        functools.partial(gram_kernel, first_layout, count, half),
        [(sweeps, half, span), message, message],
        *first, current, flops=5 * unit,
    )
    inside_route = [(i, i ^ 1) for i in range(rows)]
    outside_route = [(i, i + 1) for i in range(1, rows - 1, 2)]
    outside_route += [(target, source) for source, target in outside_route]
    outer_got = lax.ppermute(outer, "row", outside_route)
    inner_got = lax.ppermute(inner, "row", inside_route)
    straddle_high, straddle_low, raw = call(
        functools.partial(between_kernel, half),
        half_pairs(2) + [(3, columns, half)],
        current, wide_straddle, flops=4 * unit,
    )
    wide_aligned, high, low, seen = call(
        functools.partial(aligned_kernel, second_layout, count, half),
        [(sweeps, half, span)] + half_pairs(11) + [(2, columns, half)],
        *second, current, wide_straddle, flops=40 * unit,
    )
    step, up, state, sight, factor, _ = call(
        functools.partial(local_kernel, columns, half),
        [
            (3 * half + 2 * columns, half), (reach, half), (reach, 3 * half), (reach, half),
            (3, half, half), (2, 2, half, half),
        ],
        inner, inner_got, outer, outer_got, high, low, seen,
        straddle_high, straddle_low, raw, flops=40 * unit,
    )
    step_got = lax.ppermute(step, "row", inside_route)
    up_got = lax.ppermute(up, "row", [(i, i + 1) for i in range(rows - 1)])
    (start,) = call(
        functools.partial(start_kernel, half), [(part, span)], step, step_got, flops=2 * unit
    )
    chain_high, chain_low = call(
        functools.partial(chain_kernel, half), half_pairs(3), step, step_got,
        flops=4 * unit,
    )
    (local,) = call(
        functools.partial(sweep_kernel, half), [(reach + half, span)],
        current, up, state, sight, factor, high, low, wide_straddle, wide_aligned,
        flops=20 * unit,
    )
    base, *reply = call(
        functools.partial(response_kernel, half),
        [(columns, span)] + [jax.ShapeDtypeStruct((span, span), BF16)] * 2,
        step, step_got, up_got, local, factor, wide_straddle, flops=20 * unit,
    )
    carry, got, kept = start, jnp.zeros_like(start), jnp.zeros_like(start)
    for hop, route in enumerate(hop_routes(chips), 1):
        got = lax.ppermute(carry, "row", route)
        if hop < chips - 1:
            carry, kept = call(
                functools.partial(hop_kernel, half, chips - 1 - hop),
                [(part, span), (part, span)],
                start, chain_high, chain_low, got, kept, flops=unit,
            )
    other_kept = lax.ppermute(kept, "row", inside_route)
    other = lax.ppermute(got, "row", inside_route)
    (result,) = call(
        final_kernel, [(span, columns)], got, other, kept, other_kept, base, *reply,
        flops=4 * unit,
    )
    return result


def solution(mesh):
    placed = (P("row", "col"), P(None, "row", "col"), P(None, "row", "col"))

    return jax.shard_map(
        on_device, mesh=mesh, in_specs=placed, out_specs=P("row", "col"), check_vma=False
    )
```
